512 devices in a mesh: ctx: 32 (over z, x), head: 16 (over y, core).
Axes of the slice: x: 4, y: 8, z: 8, core: 2. Of those that a mesh axis runs over, the one named last changes fastest.
Arguments:
- queries: bfloat16 [16384, 4096], P(('ctx', 'head')), may hold values from -64 to 64
- keys: bfloat16 [16384, 4096], P(('ctx', 'head')), may hold values from -8 to 8
- values: bfloat16 [16384, 4096], P(('ctx', 'head')), may hold values from -6 to 6
Outputs:
- attended: bfloat16 [16384, 4096], P(('ctx', 'head'))
The draws below stay inside these ranges and needn't reach their ends.
All inputs are finite; a program needn't handle non-finite values.
Results may differ from the reference program's by a relative error of at most 0.0045.
Values may be sent and summed in bfloat16 or wider, within the bound.
No kernel may reach another device: no remote copies, remote signals or barrier semaphores. Data moves between devices by JAX's collectives and lax.ppermute only.
A program may use at most 64 MiB of HBM per device.

```python
import jax
import jax.numpy as jnp
from jax import lax

HEAD_SIZE = 128
BLOCK = 256
SUM = 16
BAND_REACH = 1024
TOK_DEV = 512
SEQ = 16384
HEAD_COUNT = 32


def pair_draw(key):
    width = HEAD_COUNT * HEAD_SIZE
    key_k = jax.random.fold_in(key, 11)
    key_q = jax.random.fold_in(key, 12)
    keys_arr = jnp.clip(jax.random.normal(key_k, (SEQ, width), jnp.float32), -6.0, 6.0)
    queries_arr = 1.5 * jnp.clip(jax.random.normal(key_q, (SEQ, width), jnp.float32), -6.0, 6.0)
    return (queries_arr, keys_arr)


def draw_queries(key, part):
    return pair_draw(key)[0].astype(jnp.bfloat16)


def draw_keys(key, part):
    return pair_draw(key)[1].astype(jnp.bfloat16)


def block_scale(own_key, shape, pieces, low, high):
    loudness = 1.0
    for axis_at, parts in pieces:
        draws = jax.random.uniform(jax.random.fold_in(jax.random.fold_in(own_key, 6), axis_at), (parts,), jnp.float32, low / len(pieces), high / len(pieces))
        loudness = loudness * jnp.repeat(jnp.exp(draws), shape[axis_at] // parts).reshape((-1,) + (1,) * (len(shape) - 1 - axis_at))
    return loudness


def scatter_about(key, dims, scale, bound, split=(), held_as=jnp.bfloat16):
    values = jax.random.normal(key, dims, jnp.float32) * scale
    if len(split) > 0:
        values = block_scale(key, dims, split, -0.22, 0.18) * values
    return jnp.clip(values, min=-bound, max=bound).astype(held_as)


def setup_inputs(seed: int = 0) -> dict:
    seeds = jax.random.split(jax.random.key(seed), 4)
    queries = draw_queries(jax.random.fold_in(seeds[3], 71), 0)
    keys = draw_keys(jax.random.fold_in(seeds[3], 71), 0)
    values = scatter_about(seeds[2], (SEQ, HEAD_COUNT * HEAD_SIZE), 1.0, 6.0, ((0, 512),))
    return {"queries": queries, "keys": keys, "values": values}


def attend_block(qblk, kb, value_block, ks, vs, start_index, spos):
    query_rows = qblk.shape[0]
    scale = HEAD_SIZE ** -0.5
    qpos = start_index + jnp.arange(query_rows, dtype=jnp.int32)
    bpos = start_index - BAND_REACH + jnp.arange(kb.shape[0], dtype=jnp.int32)
    sb = jnp.einsum('qhd,khd->hqk', qblk.astype(jnp.float32), kb.astype(jnp.float32)) * scale
    ss = jnp.einsum('qhd,khd->hqk', qblk.astype(jnp.float32), ks.astype(jnp.float32)) * scale
    diff = qpos[:, None] - bpos[None, :]
    band_ok = (bpos[None, :] >= 0) & (diff >= 0) & (diff < BAND_REACH)
    sdiff = qpos[:, None] - spos[None, :]
    sum_ok = sdiff >= BAND_REACH
    sb = jnp.where(band_ok[None], sb, -1e30)
    ss = jnp.where(sum_ok[None], ss, -1e30)
    top = jnp.maximum(jnp.max(sb, axis=-1), jnp.max(ss, axis=-1))
    pb = jnp.where(band_ok[None], jnp.exp(sb - top[..., None]), 0.0)
    ps = jnp.where(sum_ok[None], jnp.exp(ss - top[..., None]), 0.0)
    total = jnp.sum(pb, axis=-1) + jnp.sum(ps, axis=-1)
    pb_low = lax.optimization_barrier(pb.astype(jnp.bfloat16)).astype(jnp.float32)
    ps_low = lax.optimization_barrier(ps.astype(jnp.bfloat16)).astype(jnp.float32)
    numer = jnp.einsum('hqk,khd->hqd', pb_low, value_block.astype(jnp.float32))
    numer = numer + jnp.einsum('hqk,khd->hqd', ps_low, vs.astype(jnp.float32))
    result = (numer / total[..., None]).astype(jnp.bfloat16)
    return jnp.transpose(result, (1, 0, 2))


def reference(queries, keys, values):
    q_all = queries.reshape(SEQ, HEAD_COUNT, HEAD_SIZE)
    k_all = keys.reshape(SEQ, HEAD_COUNT, HEAD_SIZE)
    value_rows_all = values.reshape(SEQ, HEAD_COUNT, HEAD_SIZE)
    ks = k_all.reshape(SEQ // BLOCK, BLOCK, HEAD_COUNT, HEAD_SIZE)[:, BLOCK - SUM:].reshape(-1, HEAD_COUNT, HEAD_SIZE)
    vs = value_rows_all.reshape(SEQ // BLOCK, BLOCK, HEAD_COUNT, HEAD_SIZE)[:, BLOCK - SUM:].reshape(-1, HEAD_COUNT, HEAD_SIZE)
    ridx = jnp.arange(ks.shape[0], dtype=jnp.int32)
    spos = (ridx // SUM) * BLOCK + BLOCK - SUM + ridx % SUM
    kpad = jnp.concatenate([jnp.zeros((BAND_REACH, HEAD_COUNT, HEAD_SIZE), jnp.bfloat16), k_all], axis=0)
    value_padded = jnp.concatenate([jnp.zeros((BAND_REACH, HEAD_COUNT, HEAD_SIZE), jnp.bfloat16), value_rows_all], axis=0)
    query_rows = min(512, TOK_DEV)

    def one_block(index):
        start_index = (index * query_rows).astype(jnp.int32)
        qblk = lax.dynamic_slice_in_dim(q_all, start_index, query_rows, 0)
        kb = lax.dynamic_slice_in_dim(kpad, start_index, BAND_REACH + query_rows, 0)
        value_block = lax.dynamic_slice_in_dim(value_padded, start_index, BAND_REACH + query_rows, 0)
        return attend_block(qblk, kb, value_block, ks, vs, start_index, spos)

    blocks = lax.map(one_block, jnp.arange(SEQ // query_rows, dtype=jnp.int32))
    return blocks.reshape(SEQ, HEAD_COUNT * HEAD_SIZE)
```

```python
import functools

import jax
import jax.numpy as jnp
from jax import lax
from jax.experimental import pallas as pl
from jax.experimental.pallas import tpu as pltpu
from jax.sharding import Mesh
from jax.sharding import PartitionSpec as P

HEAD_SIZE = 128
BLOCK = 256
SUM = 16
BAND_REACH = 1024
AXES = ("z", "x", "y", "core")
PLANE = ("x", "y")
ROWS = 32
HEADS = 32
SPAN = 2 * ROWS
SRC = 32
BACK = BAND_REACH // SPAN
TILE = 8
MASKED = -1e30
VMEM = pl.BlockSpec(memory_space=pltpu.VMEM)


def pack_kernel(k_ref, v_ref, q_ref, out_ref):
    for head in range(HEADS):
        cols = slice(head * HEAD_SIZE, (head + 1) * HEAD_SIZE)
        out_ref[head, 0:ROWS, :] = k_ref[:, cols]
        out_ref[head, ROWS:2 * ROWS, :] = v_ref[:, cols]
        out_ref[head, 2 * ROWS:, :] = q_ref[:, cols]


def unpack_kernel(in_ref, out_ref):
    for head in range(HEADS):
        out_ref[:, head * HEAD_SIZE:(head + 1) * HEAD_SIZE] = in_ref[head]


def attend_kernel(place_ref, own_ref, other_ref, back_ref, back_other_ref, sum_ref, out_ref):
    plane, core = place_ref[0], place_ref[1]
    near = ((back_ref, own_ref, core), (back_other_ref, other_ref, 1 - core))
    log2e = 1.4426950408889634
    scale = HEAD_SIZE ** -0.5 * log2e
    tile_rows = TILE * ROWS

    def rows_at(start, offset):
        r = lax.broadcasted_iota(jnp.int32, (tile_rows, 1), 0)
        return (r // ROWS) * SPAN + r % ROWS + start * SPAN + offset

    def cols_at(count, start, offset):
        c = lax.broadcasted_iota(jnp.int32, (1, count), 1)
        return (c // ROWS) * SPAN + c % ROWS + start * SPAN + offset

    def score(q, k):
        return lax.dot_general(q, k, (((1,), (1,)), ((), ())), preferred_element_type=jnp.float32)

    for tile in range(SRC // TILE):
        first = tile * TILE
        q = own_ref[first:first + TILE, 2 * ROWS:, :].reshape(tile_rows, HEAD_SIZE)
        qpos = rows_at(first, core * ROWS)
        reach = jnp.minimum(BAND_REACH, plane * (SRC * SPAN) + qpos + 1)
        parts = []
        for behind, here, parity in near:
            for start in range(first - BACK, first + TILE, TILE):
                source = here if start >= 0 else behind
                at = start if start >= 0 else start + BACK
                k = source[at:at + TILE, 0:ROWS, :].reshape(tile_rows, HEAD_SIZE)
                v = source[at:at + TILE, ROWS:2 * ROWS, :].reshape(tile_rows, HEAD_SIZE)
                s = score(q, k)
                diff = qpos - cols_at(tile_rows, start, parity * ROWS)
                if start == first:
                    s = jnp.where(diff >= 0, s, MASKED)
                elif start < 0 or start == first - BACK:
                    s = jnp.where(diff < reach, s, MASKED)
                parts.append((s, v))
        k = sum_ref[:, :, 0].reshape(-1, HEAD_SIZE)
        v = sum_ref[:, :, 1].reshape(-1, HEAD_SIZE)
        s = score(q, k)
        c = lax.broadcasted_iota(jnp.int32, (1, s.shape[1]), 1)
        spos = (c // SUM) * BLOCK + BLOCK - SUM + c % SUM
        far = plane * (SRC * SPAN) + qpos - BAND_REACH
        parts.append((jnp.where(spos <= far, s, MASKED), v))

        top = functools.reduce(jnp.maximum, [jnp.max(s, axis=1, keepdims=True) for s, _ in parts])
        total = jnp.zeros((tile_rows, 1), jnp.float32)
        numer = jnp.zeros((tile_rows, HEAD_SIZE), jnp.float32)
        for s, v in parts:
            weight = jnp.exp2((s - top) * scale)
            total = total + jnp.sum(weight, axis=1, keepdims=True)
            numer = numer + jnp.dot(weight.astype(jnp.bfloat16), v, preferred_element_type=jnp.float32)
        out_ref[first:first + TILE] = (numer / total).astype(jnp.bfloat16).reshape(TILE, ROWS, HEAD_SIZE)


def local(queries, keys, values):
    bf16 = jnp.bfloat16
    plane, core = lax.axis_index("z"), lax.axis_index("core")
    packed = pl.pallas_call(
        pack_kernel,
        out_shape=jax.ShapeDtypeStruct((HEADS, 3 * ROWS, HEAD_SIZE), bf16),
        in_specs=[VMEM] * 3,
        out_specs=VMEM,
    )(keys, values, queries)
    own = lax.all_to_all(packed, PLANE, 0, 0, tiled=True)
    swap = [(0, 1), (1, 0)]
    planes = lax.axis_size("z")
    pair = own[:, :2 * ROWS]
    behind = lax.ppermute(pair[SRC - BACK:], "z", [(i, i + 1) for i in range(planes - 1)])
    other = lax.ppermute(pair, "core", swap)
    behind_other = lax.ppermute(behind, "core", swap)
    step = BLOCK // SPAN
    picked = [
        jnp.stack([part[step - 1::step, ROWS - SUM:ROWS], part[step - 1::step, 2 * ROWS - SUM:]], axis=1)
        for part in (pair, other)
    ]
    mine = jnp.where(core == 1, picked[0], picked[1])
    sums = lax.all_to_all(
        jnp.broadcast_to(mine[None], (planes, *mine.shape)), "z", 0, 0, tiled=True
    )
    place = jnp.stack([plane, core]).astype(jnp.int32)
    out = pl.pallas_call(
        attend_kernel,
        out_shape=jax.ShapeDtypeStruct((SRC, ROWS, HEAD_SIZE), bf16),
        in_specs=[pl.BlockSpec(memory_space=pltpu.SMEM)] + [VMEM] * 5,
        out_specs=VMEM,
        compiler_params=pltpu.CompilerParams(vmem_limit_bytes=48 * 2**20),
    )(place, own, other, behind, behind_other, sums)
    back = lax.all_to_all(out, PLANE, 0, 0, tiled=True)
    return pl.pallas_call(
        unpack_kernel,
        out_shape=jax.ShapeDtypeStruct((ROWS, HEADS * HEAD_SIZE), bf16),
        in_specs=[VMEM],
        out_specs=VMEM,
    )(back)


def solution(mesh):
    chips = Mesh(mesh.devices.reshape(8, 4, 8, 2), AXES)
    placed = P(AXES, None)
    return jax.shard_map(
        local, mesh=chips, in_specs=(placed,) * 3, out_specs=placed, check_vma=False
    )
```

```python
import functools

import jax
import jax.numpy as jnp
import numpy as np
from jax import lax
from jax.experimental import pallas as pl
from jax.experimental.pallas import tpu as pltpu
from jax.sharding import Mesh
from jax.sharding import PartitionSpec as P

HEAD_SIZE = 128
BLOCK = 256
SUM = 16
BAND_REACH = 1024
AXES = ("z", "x", "y", "core")
PLANE = ("x", "y")
ROWS = 32
HEADS = 32
SPAN = 2 * ROWS
SRC = 32
BACK = BAND_REACH // SPAN
TILE = 8
MASKED = -1e30
MIB = 2 ** 20
VMEM = pl.BlockSpec(memory_space=pltpu.VMEM)


def pack_kernel(k_ref, v_ref, q_ref, out_ref):
    for head in range(HEADS):
        cols = slice(head * HEAD_SIZE, (head + 1) * HEAD_SIZE)
        out_ref[head, 0:ROWS, :] = k_ref[:, cols]
        out_ref[head, ROWS:2 * ROWS, :] = v_ref[:, cols]
        out_ref[head, 2 * ROWS:, :] = q_ref[:, cols]


def unpack_kernel(in_ref, out_ref):
    for head in range(HEADS):
        out_ref[:, head * HEAD_SIZE:(head + 1) * HEAD_SIZE] = in_ref[head]


def attend_kernel(place_ref, own_ref, other_ref, late_ref, late_other_ref, out_ref):
    plane, core = place_ref[0], place_ref[1]
    near = ((late_ref, own_ref, core), (late_other_ref, other_ref, 1 - core))
    pair = 2 * ROWS
    sum_from = BACK * pair
    log2e = 1.4426950408889634
    scale = HEAD_SIZE ** -0.5 * log2e
    tile_rows = TILE * ROWS

    def rows_at(start, offset):
        r = lax.broadcasted_iota(jnp.int32, (tile_rows, 1), 0)
        return (r // ROWS) * SPAN + r % ROWS + start * SPAN + offset

    def cols_at(count, start, offset):
        c = lax.broadcasted_iota(jnp.int32, (1, count), 1)
        return (c // ROWS) * SPAN + c % ROWS + start * SPAN + offset

    def score(q, k):
        return lax.dot_general(q, k, (((1,), (1,)), ((), ())), preferred_element_type=jnp.float32)

    held = jnp.where(core == 1, late_ref[sum_from:, :], late_other_ref[sum_from:, :])
    held = held.reshape(-1, 2, SRC * SPAN // BLOCK * SUM, HEAD_SIZE)
    sums = [held[:, i].reshape(-1, HEAD_SIZE) for i in range(2)]
    for tile in range(SRC // TILE):
        first = tile * TILE
        q = own_ref[first:first + TILE, 2 * ROWS:, :].reshape(tile_rows, HEAD_SIZE)
        qpos = rows_at(first, core * ROWS)
        floor = qpos - jnp.minimum(BAND_REACH, plane * (SRC * SPAN) + qpos + 1)
        parts = []
        for behind, here, parity in near:
            for start in range(first - BACK, first + TILE, TILE):
                if start >= 0:
                    both = here[start:start + TILE, :pair, :]
                else:
                    both = behind[(start + BACK) * pair:(start + BACK + TILE) * pair, :]
                    both = both.reshape(TILE, pair, HEAD_SIZE)
                k = both[:, :ROWS].reshape(tile_rows, HEAD_SIZE)
                v = both[:, ROWS:].reshape(tile_rows, HEAD_SIZE)
                s = score(q, k)
                kpos = cols_at(tile_rows, start, parity * ROWS)
                if start == first:
                    s = jnp.where(kpos <= qpos, s, MASKED)
                elif start < 0 or start == first - BACK:
                    s = jnp.where(kpos > floor, s, MASKED)
                parts.append((s, v))
        k, v = sums
        s = score(q, k)
        c = lax.broadcasted_iota(jnp.int32, (1, s.shape[1]), 1)
        spos = (c // SUM) * BLOCK + BLOCK - SUM + c % SUM
        far = plane * (SRC * SPAN) + qpos - BAND_REACH
        parts.append((jnp.where(spos <= far, s, MASKED), v))

        top = functools.reduce(jnp.maximum, [jnp.max(s, axis=1, keepdims=True) for s, _ in parts])
        total = jnp.zeros((tile_rows, 1), jnp.float32)
        numer = jnp.zeros((tile_rows, HEAD_SIZE), jnp.float32)
        for s, v in parts:
            weight = jnp.exp2((s - top) * scale)
            total = total + jnp.sum(weight, axis=1, keepdims=True)
            numer = numer + jnp.dot(weight.astype(jnp.bfloat16), v, preferred_element_type=jnp.float32)
        out_ref[first:first + TILE] = (numer / total).astype(jnp.bfloat16).reshape(TILE, ROWS, HEAD_SIZE)


def sum_groups():
    sizes = [lax.axis_size(axis) for axis in AXES]
    device = np.arange(np.prod(sizes)).reshape(sizes)
    along_z = device[..., 1].transpose(1, 2, 0).reshape(-1, sizes[0])
    along_y = device[..., 0].reshape(-1, sizes[2])
    return np.concatenate([along_z, along_y]).tolist()


def local(queries, keys, values):
    bf16 = jnp.bfloat16
    plane, core = lax.axis_index("z"), lax.axis_index("core")
    packed = pl.pallas_call(
        pack_kernel,
        out_shape=jax.ShapeDtypeStruct((HEADS, 3 * ROWS, HEAD_SIZE), bf16),
        in_specs=[VMEM] * 3,
        out_specs=VMEM,
        compiler_params=pltpu.CompilerParams(vmem_limit_bytes=62 * MIB),
    )(keys, values, queries)
    own = lax.all_to_all(packed, PLANE, 0, 0, tiled=True)
    swap = [(0, 1), (1, 0)]
    planes = lax.axis_size("z")
    pair = own[:, :2 * ROWS]
    behind = lax.ppermute(pair[SRC - BACK:], "z", [(i, i + 1) for i in range(planes - 1)])
    other = lax.ppermute(pair, "core", swap)
    step = BLOCK // SPAN
    mine = jnp.concatenate([
        own[step - 1::step, ROWS - SUM:ROWS].reshape(-1, HEAD_SIZE),
        own[step - 1::step, 2 * ROWS - SUM:2 * ROWS].reshape(-1, HEAD_SIZE),
    ])
    shares = jnp.broadcast_to(mine[None], (planes, *mine.shape))
    sums = lax.all_to_all(shares, AXES, 0, 0, axis_index_groups=sum_groups(), tiled=True)
    late = jnp.concatenate([behind.reshape(-1, HEAD_SIZE), sums.reshape(-1, HEAD_SIZE)])
    late, other = lax.optimization_barrier((late, other))
    late_other = lax.ppermute(late, "core", swap)
    place = jnp.stack([plane, core]).astype(jnp.int32)
    out = pl.pallas_call(
        attend_kernel,
        out_shape=jax.ShapeDtypeStruct((SRC, ROWS, HEAD_SIZE), bf16),
        in_specs=[pl.BlockSpec(memory_space=pltpu.SMEM)] + [VMEM] * 4,
        out_specs=VMEM,
        compiler_params=pltpu.CompilerParams(vmem_limit_bytes=32 * MIB),
    )(place, own, other, late, late_other)
    back = lax.all_to_all(out, PLANE, 0, 0, tiled=True)
    return pl.pallas_call(
        unpack_kernel,
        out_shape=jax.ShapeDtypeStruct((ROWS, HEADS * HEAD_SIZE), bf16),
        in_specs=[VMEM],
        out_specs=VMEM,
        compiler_params=pltpu.CompilerParams(vmem_limit_bytes=8 * MIB),
    )(back)


def solution(mesh):
    chips = Mesh(mesh.devices.reshape(8, 4, 8, 2), AXES)
    placed = P(AXES, None)
    return jax.shard_map(
        local, mesh=chips, in_specs=(placed,) * 3, out_specs=placed, check_vma=False
    )
```

```python
import functools

import jax
import jax.numpy as jnp
import numpy as np
from jax import lax
from jax.experimental import pallas as pl
from jax.experimental.pallas import tpu as pltpu
from jax.sharding import Mesh
from jax.sharding import PartitionSpec as P

HEAD_SIZE = 128
BLOCK = 256
SUM = 16
BAND_REACH = 1024
AXES = ("z", "x", "y", "core")
PLANE = ("x", "y")
ROWS = 32
HEADS = 32
SPAN = 2 * ROWS
SRC = 32
BACK = BAND_REACH // SPAN
TILE = 8
MASKED = -1e30
SCALE = HEAD_SIZE ** -0.5 * 1.4426950408889634
MIB = 2 ** 20
VMEM = pl.BlockSpec(memory_space=pltpu.VMEM)


def pack_kernel(k_ref, v_ref, q_ref, out_ref, held, slabs, in_sems, out_sems):
    half = HEADS // 2
    loads, stores = [], []
    for i in range(2):
        cols = pl.ds(i * half * HEAD_SIZE, half * HEAD_SIZE)
        for j, ref in enumerate((k_ref, v_ref, q_ref)):
            loads.append(pltpu.make_async_copy(ref.at[:, cols], held.at[j, :, cols], in_sems.at[i, j]))
        heads = pl.ds(i * half, half)
        stores.append(pltpu.make_async_copy(slabs.at[heads], out_ref.at[heads], out_sems.at[i]))
    for load in loads:
        load.start()
    for i in range(2):
        for j in range(3):
            loads[3 * i + j].wait()
            for head in range(i * half, (i + 1) * half):
                cols = slice(head * HEAD_SIZE, (head + 1) * HEAD_SIZE)
                slabs[head, j * ROWS:(j + 1) * ROWS, :] = held[j, :, cols]
        stores[i].start()
    for store in stores:
        store.wait()


def unpack_kernel(in_ref, out_ref):
    for head in range(HEADS):
        out_ref[:, head * HEAD_SIZE:(head + 1) * HEAD_SIZE] = in_ref[head]


def row_positions(start, offset):
    r = lax.broadcasted_iota(jnp.int32, (TILE * ROWS, 1), 0)
    return (r // ROWS) * SPAN + r % ROWS + start * SPAN + offset


def col_positions(start, offset):
    c = lax.broadcasted_iota(jnp.int32, (1, TILE * ROWS), 1)
    return (c // ROWS) * SPAN + c % ROWS + start * SPAN + offset


def score(q, k):
    return lax.dot_general(q, k, (((1,), (1,)), ((), ())), preferred_element_type=jnp.float32)


def weigh(parts, top):
    total = numer = 0.0
    for s, v in parts:
        weight = jnp.exp2((s - top) * SCALE)
        total = total + jnp.sum(weight, axis=1, keepdims=True)
        numer = numer + jnp.dot(weight.astype(jnp.bfloat16), v, preferred_element_type=jnp.float32)
    return total, numer


def here_kernel(place_ref, own_ref, other_ref, numer_ref, top_ref, total_ref):
    core = place_ref[1]
    rows = TILE * ROWS
    for tile in range(SRC // TILE):
        first = tile * TILE
        q = own_ref[first:first + TILE, 2 * ROWS:, :].reshape(rows, HEAD_SIZE)
        qpos = row_positions(first, core * ROWS)
        parts = []
        for here, parity in ((own_ref, core), (other_ref, 1 - core)):
            for start in range(max(0, first - BACK), first + TILE, TILE):
                k = here[start:start + TILE, 0:ROWS, :].reshape(rows, HEAD_SIZE)
                v = here[start:start + TILE, ROWS:2 * ROWS, :].reshape(rows, HEAD_SIZE)
                s = score(q, k)
                kpos = col_positions(start, parity * ROWS)
                if start == first:
                    s = jnp.where(kpos <= qpos, s, MASKED)
                elif start == first - BACK:
                    s = jnp.where(kpos > qpos - BAND_REACH, s, MASKED)
                parts.append((s, v))
        top = functools.reduce(jnp.maximum, [jnp.max(s, axis=1, keepdims=True) for s, _ in parts])
        total, numer = weigh(parts, top)
        at = slice(tile * rows, (tile + 1) * rows)
        numer_ref[at] = numer
        top_ref[at] = jnp.broadcast_to(top, (rows, HEAD_SIZE))
        total_ref[at] = jnp.broadcast_to(total, (rows, HEAD_SIZE))


def late_kernel(planes, place_ref, own_ref, late_ref, late_other_ref, numer_ref, top_ref, total_ref, out_ref):
    plane, core = place_ref[0], place_ref[1]
    rows, pair = TILE * ROWS, 2 * ROWS
    sum_from = BACK * pair
    per_plane = SRC * SPAN // BLOCK * SUM

    def attend(k_sum, v_sum):
        c = lax.broadcasted_iota(jnp.int32, (1, k_sum.shape[0]), 1)
        spos = (c // SUM) * BLOCK + BLOCK - SUM + c % SUM
        for tile in range(SRC // TILE):
            first = tile * TILE
            at = slice(tile * rows, (tile + 1) * rows)
            q = own_ref[first:first + TILE, 2 * ROWS:, :].reshape(rows, HEAD_SIZE)
            qpos = row_positions(first, core * ROWS)
            floor = qpos - jnp.minimum(BAND_REACH, plane * (SRC * SPAN) + qpos + 1)
            parts = []
            for behind, parity in ((late_ref, core), (late_other_ref, 1 - core)):
                for start in range(first - BACK, 0, TILE):
                    both = behind[(start + BACK) * pair:(start + BACK + TILE) * pair, :]
                    both = both.reshape(TILE, pair, HEAD_SIZE)
                    s = score(q, both[:, :ROWS].reshape(rows, HEAD_SIZE))
                    s = jnp.where(col_positions(start, parity * ROWS) > floor, s, MASKED)
                    parts.append((s, both[:, ROWS:].reshape(rows, HEAD_SIZE)))
            far = plane * (SRC * SPAN) + qpos - BAND_REACH
            parts.append((jnp.where(spos <= far, score(q, k_sum), MASKED), v_sum))
            near_top = top_ref[at]
            tops = [jnp.max(s, axis=1, keepdims=True) for s, _ in parts]
            top = functools.reduce(jnp.maximum, tops, near_top)
            total, numer = weigh(parts, top[:, :1])
            keep = jnp.exp2((near_top - top) * SCALE)
            numer = numer + keep * numer_ref[at]
            total = total + keep * total_ref[at]
            out_ref[first:first + TILE] = (numer / total).astype(jnp.bfloat16).reshape(TILE, ROWS, HEAD_SIZE)

    for level in range(2, planes + 1, 2):

        @pl.when((plane >= level - 2) & (plane < level))
        def _(level=level):
            held = slice(sum_from, sum_from + level * 2 * per_plane)
            held = jnp.where(core == 1, late_ref[held, :], late_other_ref[held, :])
            held = held.reshape(level, 2, per_plane, HEAD_SIZE)
            attend(held[:, 0].reshape(-1, HEAD_SIZE), held[:, 1].reshape(-1, HEAD_SIZE))


def sum_groups():
    sizes = [lax.axis_size(axis) for axis in AXES]
    device = np.arange(np.prod(sizes)).reshape(sizes)
    along_z = device[..., 1].transpose(1, 2, 0).reshape(-1, sizes[0])
    along_y = device[..., 0].reshape(-1, sizes[2])
    return np.concatenate([along_z, along_y]).tolist()


def local(queries, keys, values):
    bf16 = jnp.bfloat16
    plane, core = lax.axis_index("z"), lax.axis_index("core")
    packed = pl.pallas_call(
        pack_kernel,
        out_shape=jax.ShapeDtypeStruct((HEADS, 3 * ROWS, HEAD_SIZE), bf16),
        in_specs=[pl.BlockSpec(memory_space=pltpu.HBM)] * 3,
        out_specs=pl.BlockSpec(memory_space=pltpu.HBM),
        scratch_shapes=[
            pltpu.VMEM((3, ROWS, HEADS * HEAD_SIZE), bf16),
            pltpu.VMEM((HEADS, 3 * ROWS, HEAD_SIZE), bf16),
            pltpu.SemaphoreType.DMA((2, 3)),
            pltpu.SemaphoreType.DMA((2,)),
        ],
        compiler_params=pltpu.CompilerParams(vmem_limit_bytes=62 * MIB),
    )(keys, values, queries)
    own = lax.all_to_all(packed, PLANE, 0, 0, tiled=True)
    swap = [(0, 1), (1, 0)]
    planes = lax.axis_size("z")
    pair = own[:, :2 * ROWS]
    behind = lax.ppermute(pair[SRC - BACK:], "z", [(i, i + 1) for i in range(planes - 1)])
    other = lax.ppermute(pair, "core", swap)
    step = BLOCK // SPAN
    mine = jnp.concatenate([
        own[step - 1::step, ROWS - SUM:ROWS].reshape(-1, HEAD_SIZE),
        own[step - 1::step, 2 * ROWS - SUM:2 * ROWS].reshape(-1, HEAD_SIZE),
    ])
    shares = jnp.broadcast_to(mine[None], (planes, *mine.shape))
    sums = lax.all_to_all(shares, AXES, 0, 0, axis_index_groups=sum_groups(), tiled=True)
    late = jnp.concatenate([behind.reshape(-1, HEAD_SIZE), sums.reshape(-1, HEAD_SIZE)])
    late, other = lax.optimization_barrier((late, other))
    late_other = lax.ppermute(late, "core", swap)
    place = jnp.stack([plane, core]).astype(jnp.int32)
    smem = pl.BlockSpec(memory_space=pltpu.SMEM)
    part = jax.ShapeDtypeStruct((SRC * ROWS, HEAD_SIZE), jnp.float32)
    near = pl.pallas_call(
        here_kernel,
        out_shape=(part, part, part),
        in_specs=[smem] + [VMEM] * 2,
        out_specs=(VMEM,) * 3,
        compiler_params=pltpu.CompilerParams(vmem_limit_bytes=16 * MIB),
        cost_estimate=pl.CostEstimate(flops=4 * 10 ** 8, transcendentals=10 ** 6, bytes_accessed=3 * 10 ** 6),
    )(place, own, other)
    out = pl.pallas_call(
        functools.partial(late_kernel, planes),
        out_shape=jax.ShapeDtypeStruct((SRC, ROWS, HEAD_SIZE), bf16),
        in_specs=[smem] + [VMEM] * 6,
        out_specs=VMEM,
        compiler_params=pltpu.CompilerParams(vmem_limit_bytes=16 * MIB),
    )(place, own, late, late_other, *near)
    back = lax.all_to_all(out, PLANE, 0, 0, tiled=True)
    return pl.pallas_call(
        unpack_kernel,
        out_shape=jax.ShapeDtypeStruct((ROWS, HEADS * HEAD_SIZE), bf16),
        in_specs=[VMEM],
        out_specs=VMEM,
        compiler_params=pltpu.CompilerParams(vmem_limit_bytes=8 * MIB),
    )(back)


def solution(mesh):
    chips = Mesh(mesh.devices.reshape(8, 4, 8, 2), AXES)
    placed = P(AXES, None)
    return jax.shard_map(
        local, mesh=chips, in_specs=(placed,) * 3, out_specs=placed, check_vma=False
    )
```

```python
import functools

import jax
import jax.numpy as jnp
import numpy as np
from jax import lax
from jax.experimental import pallas as pl
from jax.experimental.pallas import tpu as pltpu
from jax.sharding import Mesh
from jax.sharding import PartitionSpec as P

HEAD_SIZE = 128
BLOCK = 256
SUM = 16
BAND_REACH = 1024
AXES = ("z", "x", "y", "core")
PLANE = ("x", "y")
ROWS = 32
HEADS = 32
SPAN = 2 * ROWS
SRC = 32
BACK = BAND_REACH // SPAN
TILE = 8
MASKED = -1e30
SCALE = HEAD_SIZE ** -0.5 * 1.4426950408889634
MIB = 2 ** 20
VMEM = pl.BlockSpec(memory_space=pltpu.VMEM)


def pack_kernel(k_ref, v_ref, q_ref, out_ref, held, slabs, in_sems, out_sems):
    half = HEADS // 2
    loads, stores = [], []
    for i in range(2):
        cols = pl.ds(i * half * HEAD_SIZE, half * HEAD_SIZE)
        for j, ref in enumerate((k_ref, v_ref, q_ref)):
            loads.append(pltpu.make_async_copy(ref.at[:, cols], held.at[j, :, cols], in_sems.at[i, j]))
        heads = pl.ds(i * half, half)
        stores.append(pltpu.make_async_copy(slabs.at[heads], out_ref.at[heads], out_sems.at[i]))
    for load in loads:
        load.start()
    for i in range(2):
        for j in range(3):
            loads[3 * i + j].wait()
            for head in range(i * half, (i + 1) * half):
                cols = slice(head * HEAD_SIZE, (head + 1) * HEAD_SIZE)
                slabs[head, j * ROWS:(j + 1) * ROWS, :] = held[j, :, cols]
        stores[i].start()
    for store in stores:
        store.wait()


def unpack_kernel(in_ref, out_ref):
    for head in range(HEADS):
        out_ref[:, head * HEAD_SIZE:(head + 1) * HEAD_SIZE] = in_ref[head]


def row_positions(start, offset):
    r = lax.broadcasted_iota(jnp.int32, (TILE * ROWS, 1), 0)
    return (r // ROWS) * SPAN + r % ROWS + start * SPAN + offset


def col_positions(start, offset):
    c = lax.broadcasted_iota(jnp.int32, (1, TILE * ROWS), 1)
    return (c // ROWS) * SPAN + c % ROWS + start * SPAN + offset


def score(q, k):
    return lax.dot_general(q, k, (((1,), (1,)), ((), ())), preferred_element_type=jnp.float32)


def weigh(parts, top):
    total = numer = 0.0
    for s, v in parts:
        weight = jnp.exp2((s - top) * SCALE)
        total = total + jnp.sum(weight, axis=1, keepdims=True)
        numer = numer + jnp.dot(weight.astype(jnp.bfloat16), v, preferred_element_type=jnp.float32)
    return total, numer


def here_kernel(place_ref, own_ref, other_ref, numer_ref, top_ref, total_ref):
    core = place_ref[1]
    rows = TILE * ROWS
    for tile in range(SRC // TILE):
        first = tile * TILE
        q = own_ref[first:first + TILE, 2 * ROWS:, :].reshape(rows, HEAD_SIZE)
        qpos = row_positions(first, core * ROWS)
        parts = []
        for here, parity in ((own_ref, core), (other_ref, 1 - core)):
            for start in range(max(0, first - BACK), first + TILE, TILE):
                k = here[start:start + TILE, 0:ROWS, :].reshape(rows, HEAD_SIZE)
                v = here[start:start + TILE, ROWS:2 * ROWS, :].reshape(rows, HEAD_SIZE)
                s = score(q, k)
                kpos = col_positions(start, parity * ROWS)
                if start == first:
                    s = jnp.where(kpos <= qpos, s, MASKED)
                elif start == first - BACK:
                    s = jnp.where(kpos > qpos - BAND_REACH, s, MASKED)
                parts.append((s, v))
        top = functools.reduce(jnp.maximum, [jnp.max(s, axis=1, keepdims=True) for s, _ in parts])
        total, numer = weigh(parts, top)
        at = slice(tile * rows, (tile + 1) * rows)
        numer_ref[at] = numer
        top_ref[at] = jnp.broadcast_to(top, (rows, HEAD_SIZE))
        total_ref[at] = jnp.broadcast_to(total, (rows, HEAD_SIZE))


def late_kernel(planes, place_ref, own_ref, late_ref, late_other_ref, numer_ref, top_ref, total_ref, out_ref):
    plane, core = place_ref[0], place_ref[1]
    rows, pair = TILE * ROWS, 2 * ROWS
    sum_from = BACK * pair
    per_plane = SRC * SPAN // BLOCK * SUM

    def attend(k_sum, v_sum, first_plane):
        c = lax.broadcasted_iota(jnp.int32, (1, k_sum.shape[0]), 1)
        spos = (c // SUM) * BLOCK + BLOCK - SUM + c % SUM
        for tile in range(SRC // TILE):
            first = tile * TILE
            at = slice(tile * rows, (tile + 1) * rows)
            q = own_ref[first:first + TILE, 2 * ROWS:, :].reshape(rows, HEAD_SIZE)
            qpos = row_positions(first, core * ROWS)
            floor = qpos - jnp.minimum(BAND_REACH, plane * (SRC * SPAN) + qpos + 1)
            parts = []
            for behind, parity in ((late_ref, core), (late_other_ref, 1 - core)):
                for start in () if first_plane else range(first - BACK, 0, TILE):
                    both = behind[(start + BACK) * pair:(start + BACK + TILE) * pair, :]
                    both = both.reshape(TILE, pair, HEAD_SIZE)
                    s = score(q, both[:, :ROWS].reshape(rows, HEAD_SIZE))
                    s = jnp.where(col_positions(start, parity * ROWS) > floor, s, MASKED)
                    parts.append((s, both[:, ROWS:].reshape(rows, HEAD_SIZE)))
            far = plane * (SRC * SPAN) + qpos - BAND_REACH
            parts.append((jnp.where(spos <= far, score(q, k_sum), MASKED), v_sum))
            near_top = top_ref[at]
            tops = [jnp.max(s, axis=1, keepdims=True) for s, _ in parts]
            top = functools.reduce(jnp.maximum, tops, near_top)
            total, numer = weigh(parts, top[:, :1])
            keep = jnp.exp2((near_top - top) * SCALE)
            numer = numer + keep * numer_ref[at]
            total = total + keep * total_ref[at]
            out_ref[first:first + TILE] = (numer / total).astype(jnp.bfloat16).reshape(TILE, ROWS, HEAD_SIZE)

    for level in range(1, planes + 1):

        @pl.when(plane == level - 1)
        def _(level=level):
            held = slice(sum_from, sum_from + level * 2 * per_plane)
            held = jnp.where(core == 1, late_ref[held, :], late_other_ref[held, :])
            held = held.reshape(level, 2, per_plane, HEAD_SIZE)
            attend(held[:, 0].reshape(-1, HEAD_SIZE), held[:, 1].reshape(-1, HEAD_SIZE), level == 1)


def sum_groups():
    sizes = [lax.axis_size(axis) for axis in AXES]
    device = np.arange(np.prod(sizes)).reshape(sizes)
    along_z = device[..., 1].transpose(1, 2, 0).reshape(-1, sizes[0])
    along_y = device[..., 0].reshape(-1, sizes[2])
    return np.concatenate([along_z, along_y]).tolist()


def local(queries, keys, values):
    bf16 = jnp.bfloat16
    plane, core = lax.axis_index("z"), lax.axis_index("core")
    packed = pl.pallas_call(
        pack_kernel,
        out_shape=jax.ShapeDtypeStruct((HEADS, 3 * ROWS, HEAD_SIZE), bf16),
        in_specs=[pl.BlockSpec(memory_space=pltpu.HBM)] * 3,
        out_specs=pl.BlockSpec(memory_space=pltpu.HBM),
        scratch_shapes=[
            pltpu.VMEM((3, ROWS, HEADS * HEAD_SIZE), bf16),
            pltpu.VMEM((HEADS, 3 * ROWS, HEAD_SIZE), bf16),
            pltpu.SemaphoreType.DMA((2, 3)),
            pltpu.SemaphoreType.DMA((2,)),
        ],
        compiler_params=pltpu.CompilerParams(vmem_limit_bytes=62 * MIB),
    )(keys, values, queries)
    own = lax.all_to_all(packed, PLANE, 0, 0, tiled=True)
    swap = [(0, 1), (1, 0)]
    planes = lax.axis_size("z")
    pair = own[:, :2 * ROWS]
    behind = lax.ppermute(pair[SRC - BACK:], "z", [(i, i + 1) for i in range(planes - 1)])
    other = lax.ppermute(pair, "core", swap)
    step = BLOCK // SPAN
    mine = jnp.concatenate([
        own[step - 1::step, ROWS - SUM:ROWS].reshape(-1, HEAD_SIZE),
        own[step - 1::step, 2 * ROWS - SUM:2 * ROWS].reshape(-1, HEAD_SIZE),
    ])
    shares = jnp.broadcast_to(mine[None], (planes, *mine.shape))
    sums = lax.all_to_all(shares, AXES, 0, 0, axis_index_groups=sum_groups(), tiled=True)
    late = jnp.concatenate([behind.reshape(-1, HEAD_SIZE), sums.reshape(-1, HEAD_SIZE)])
    late, other = lax.optimization_barrier((late, other))
    late_other = lax.ppermute(late, "core", swap)
    place = jnp.stack([plane, core]).astype(jnp.int32)
    smem = pl.BlockSpec(memory_space=pltpu.SMEM)
    part = jax.ShapeDtypeStruct((SRC * ROWS, HEAD_SIZE), jnp.float32)
    near = pl.pallas_call(
        here_kernel,
        out_shape=(part, part, part),
        in_specs=[smem] + [VMEM] * 2,
        out_specs=(VMEM,) * 3,
        compiler_params=pltpu.CompilerParams(vmem_limit_bytes=16 * MIB),
        cost_estimate=pl.CostEstimate(flops=4 * 10 ** 8, transcendentals=10 ** 6, bytes_accessed=3 * 10 ** 6),
    )(place, own, other)
    out = pl.pallas_call(
        functools.partial(late_kernel, planes),
        out_shape=jax.ShapeDtypeStruct((SRC, ROWS, HEAD_SIZE), bf16),
        in_specs=[smem] + [VMEM] * 6,
        out_specs=VMEM,
        compiler_params=pltpu.CompilerParams(vmem_limit_bytes=16 * MIB),
    )(place, own, late, late_other, *near)
    back = lax.all_to_all(out, PLANE, 0, 0, tiled=True)
    return pl.pallas_call(
        unpack_kernel,
        out_shape=jax.ShapeDtypeStruct((ROWS, HEADS * HEAD_SIZE), bf16),
        in_specs=[VMEM],
        out_specs=VMEM,
        compiler_params=pltpu.CompilerParams(vmem_limit_bytes=8 * MIB),
    )(back)


def solution(mesh):
    chips = Mesh(mesh.devices.reshape(8, 4, 8, 2), AXES)
    placed = P(AXES, None)
    return jax.shard_map(
        local, mesh=chips, in_specs=(placed,) * 3, out_specs=placed, check_vma=False
    )
```
